128 devices in a mesh: gx: 4 (over x), gy: 32 (over z, y, core).
Axes of the slice: x: 4, y: 4, z: 4, core: 2. Of those that a mesh axis runs over, the one named last changes fastest.
Arguments:
- gcm_state: float32 [3, 58, 16384], P(None, None, ('gx', 'gy')), may hold values from -4 to 4
- crm_state: float32 [2, 58, 524288], P(None, None, ('gx', 'gy')), may hold values from -4 to 4
- send_source: int32 [16384], P(('gx', 'gy')), may hold values from 0 to 127, as said below
- group_owner: int32 [4096], P(('gx', 'gy')), may hold values from 0 to 31, as said below
Outputs:
- tendency: float32 [2, 58, 16384], P(None, None, ('gx', 'gy'))
- crm_next: float32 [2, 58, 1048576], P(None, None, ('gx', 'gy'))
The draws below stay inside these ranges and needn't reach their ends.
Inputs may be any that keep to these rules, and one draw needn't show every extreme that they name: `send_source`: each aligned block of 128 entries is a permutation of 0 to 127. `group_owner`: A home device gives at most 2 groups to one owner; in every draw one owner in each gx row receives 2 groups from every home of its row.
All inputs are finite; a program needn't handle non-finite values.
Results may differ from the reference program's by a relative error of at most 0.0001.
Values sent between devices are 32-bit elements; how exact they have to be, the bound alone decides.
A program may use at most 256 MiB of HBM per device.

```python
import jax
import jax.numpy as jnp
from jax import lax

CRM_X = 32
CRM_LEV = 58
GROUP = 4
SUBSTEPS = 1
ADJ_ITERS = 3
COLS_DEV = 128
COLUMNS = 16384
PER_PEER = 1
GROUPS_DEV = 32
NCHUNKS = 4096
PAIR_CAP = 2
OWN_SLOTS = 64
HOME_LANES = 524288
OWN_LANES = 1048576
N_GX = 4
N_GY = 32


def draw_send_source(key, part):
    block_count = COLUMNS // COLS_DEV
    block_keys = jax.random.split(key, block_count)

    def one_block(single_key):
        return jax.random.permutation(single_key, COLS_DEV)
    return jax.vmap(one_block)(block_keys).reshape(COLUMNS).astype(jnp.int32)


def draw_group_owner(key, part):
    gy_count = OWN_SLOTS // PAIR_CAP
    home_count = NCHUNKS // GROUPS_DEV
    row_count = home_count // gy_count
    key_hot, key_bias, key_noise, key_order = jax.random.split(key, 4)
    hot_owner = jax.random.randint(key_hot, (row_count,), 0, gy_count, dtype=jnp.int32)
    owner_bias = jax.random.randint(key_bias, (row_count, gy_count), 0, 1 << 17, dtype=jnp.int32)
    slot_noise = jax.random.randint(key_noise, (home_count, OWN_SLOTS), 0, 1 << 17, dtype=jnp.int32)
    slot_ids = jnp.arange(OWN_SLOTS, dtype=jnp.int32)
    slot_owner = slot_ids // PAIR_CAP
    home_row = jnp.arange(home_count, dtype=jnp.int32) // gy_count
    is_hot = (slot_owner[None, :] == hot_owner[home_row][:, None]).astype(jnp.int32)
    score = slot_noise + owner_bias[home_row][:, slot_owner] + is_hot * (1 << 20)
    score = score * OWN_SLOTS + slot_ids[None, :]
    top_scores, chosen = lax.top_k(score, GROUPS_DEV)
    order_keys = jax.random.split(key_order, home_count)

    def shuffle_row(single_key, chosen_row):
        return chosen_row[jax.random.permutation(single_key, GROUPS_DEV)]
    shuffled = jax.vmap(shuffle_row)(order_keys, chosen)
    return (shuffled // PAIR_CAP).reshape(NCHUNKS).astype(jnp.int32)


def steps_of(rng, dims, shards, smallest, top_value):
    factor_of = 1.0
    for dim, shards_of in shards:
        steps = jax.random.uniform(jax.random.fold_in(jax.random.fold_in(rng, 6), dim), (shards_of,), jnp.float32, smallest / len(shards), top_value / len(shards))
        factor_of = factor_of * jnp.repeat(jnp.exp(steps), dims[dim] // shards_of).reshape((-1,) + (1,) * (len(dims) - 1 - dim))
    return factor_of


def noise(rng, shape, width, limit, pieces=(), held_as=jnp.bfloat16):
    drawn = jax.random.normal(rng, shape, jnp.float32) * width
    if len(pieces) > 0:
        drawn = steps_of(rng, shape, pieces, -0.22, 0.18) * drawn
    return jnp.clip(drawn, min=-limit, max=limit).astype(held_as)


def setup_inputs(seed: int = 0) -> dict:
    keys = jax.random.split(jax.random.key(seed), 5)
    return {
        "gcm_state": noise(keys[0], (3, CRM_LEV, COLUMNS), 1.0, 4.0, ((2, 128),), jnp.float32),
        "crm_state": noise(keys[1], (2, CRM_LEV, HOME_LANES), 1.0, 4.0, ((2, 128),), jnp.float32),
        "send_source": draw_send_source(jax.random.fold_in(keys[4], 71), 0),
        "group_owner": draw_group_owner(jax.random.fold_in(keys[4], 71), 0),
    }


courant_scale = 0.25
diffuse_across = 0.1
diffuse_vertical = 0.1
relax_rate = 0.5
condensation_warming_factor = 2.5
autoconversion = 0.2


def crm_advance(fine_grid_variables, coarse_grid_variables):
    lane_count = fine_grid_variables.shape[2]
    column_count = coarse_grid_variables.shape[2]
    x_index = lax.broadcasted_iota(jnp.int32, (1, 1, lane_count), 2) % CRM_X

    def spread_lanes(values):
        shaped = jnp.broadcast_to(values[..., None], values.shape + (CRM_X,))
        return shaped.reshape(values.shape[:-1] + (lane_count,))

    def height_mean_profile(values):
        return jnp.mean(values.reshape(values.shape[:-1] + (column_count, CRM_X)), axis=-1)

    speed = spread_lanes(courant_scale * jnp.tanh(coarse_grid_variables[2]))[None]
    target = coarse_grid_variables[0:2]
    present_snapshot = fine_grid_variables
    kelvin_reading = fine_grid_variables[0]
    for substep in range(SUBSTEPS):
        west_cells = jnp.where(x_index == 0, jnp.roll(present_snapshot, -(CRM_X - 1), axis=2), jnp.roll(present_snapshot, 1, axis=2))
        east_cells = jnp.where(x_index == CRM_X - 1, jnp.roll(present_snapshot, CRM_X - 1, axis=2), jnp.roll(present_snapshot, -1, axis=2))
        lower_cells = jnp.concatenate([present_snapshot[:, :1], present_snapshot[:, :-1]], axis=1)
        upper_cells = jnp.concatenate([present_snapshot[:, 1:], present_snapshot[:, -1:]], axis=1)
        updated = (present_snapshot - 0.5 * speed * (east_cells - west_cells)
                   + diffuse_across * (east_cells - 2.0 * present_snapshot + west_cells)
                   + diffuse_vertical * (upper_cells - 2.0 * present_snapshot + lower_cells))
        updated = updated + relax_rate * spread_lanes(target - height_mean_profile(updated))
        dry_enthalpy_measure = updated[0]
        moisture_mixing_fraction = updated[1]
        kelvin_reading = dry_enthalpy_measure
        for sweep in range(ADJ_ITERS):
            kelvin_reading = dry_enthalpy_measure + condensation_warming_factor * (moisture_mixing_fraction - jax.nn.sigmoid(kelvin_reading))
        condensed_droplet_mass = moisture_mixing_fraction - jax.nn.sigmoid(kelvin_reading)
        moisture_mixing_fraction = moisture_mixing_fraction - autoconversion * condensed_droplet_mass
        present_snapshot = jnp.stack([dry_enthalpy_measure, moisture_mixing_fraction])
    time_derivative_values = jnp.stack([height_mean_profile(kelvin_reading) - coarse_grid_variables[0], height_mean_profile(present_snapshot[1]) - coarse_grid_variables[1]])
    return present_snapshot, time_derivative_values


def advance_block(paired):
    return crm_advance(paired[0], paired[1])


def reference(gcm_state, crm_state, send_source, group_owner):
    device_count = N_GX * N_GY
    positions = jnp.arange(COLUMNS, dtype=jnp.int32)
    source_dev = positions // COLS_DEV
    inside = positions % COLS_DEV
    dyn_index = (source_dev * COLS_DEV + send_source).astype(jnp.int32)
    phys_index = ((inside // PER_PEER) * COLS_DEV + source_dev * PER_PEER + inside % PER_PEER).astype(jnp.int32)
    gcm_phys = jnp.zeros_like(gcm_state).at[:, :, phys_index].set(gcm_state[:, :, dyn_index])
    crm_blocks = crm_state.reshape(2, CRM_LEV, device_count, COLS_DEV * CRM_X).transpose(2, 0, 1, 3)
    gcm_blocks = gcm_phys.reshape(3, CRM_LEV, device_count, COLS_DEV).transpose(2, 0, 1, 3)
    new_blocks, tend_blocks = lax.map(advance_block, (crm_blocks, gcm_blocks))
    tend_phys = tend_blocks.transpose(1, 2, 0, 3).reshape(2, CRM_LEV, COLUMNS)
    tendency = jnp.zeros_like(tend_phys).at[:, :, dyn_index].set(tend_phys[:, :, phys_index])
    owners = group_owner.reshape(device_count, GROUPS_DEV)
    group_ids = jnp.arange(GROUPS_DEV, dtype=jnp.int32)
    earlier = group_ids[None, :] < group_ids[:, None]
    same_owner = owners[:, :, None] == owners[:, None, :]
    group_ranks = jnp.sum(jnp.logical_and(same_owner, earlier[None]), axis=2).astype(jnp.int32)
    homes = jnp.arange(device_count, dtype=jnp.int32)[:, None]
    slot_index = ((homes // N_GY) * N_GY + owners) * OWN_SLOTS + (homes % N_GY) * PAIR_CAP + group_ranks
    lane_group = GROUP * CRM_X
    groups = new_blocks.reshape(device_count, 2, CRM_LEV, GROUPS_DEV, lane_group).transpose(1, 2, 0, 3, 4)
    groups = groups.reshape(2, CRM_LEV, device_count * GROUPS_DEV, lane_group)
    placed = jnp.zeros((2, CRM_LEV, device_count * OWN_SLOTS, lane_group), jnp.float32)
    placed = placed.at[:, :, slot_index.reshape(-1).astype(jnp.int32)].set(groups)
    crm_next = placed.reshape(2, CRM_LEV, OWN_LANES)
    return tendency, crm_next
```

```python
import functools

import jax
import jax.numpy as jnp
from jax import lax
from jax.experimental import pallas as pl
from jax.experimental.pallas import tpu as pltpu
from jax.sharding import PartitionSpec as P

CRM_X = 32
LEV = 58
PAD = 64
LANES = 128
NX = 4
NY = 32
GROUPS = 32
F32 = jnp.float32
BF16 = jnp.bfloat16
MESH = pl.DeviceIdType.MESH

NN = (((1,), (0,)), ((), ()))
NT = (((1,), (1,)), ((), ()))

OFFSETS = [(a, b, c) for a in range(4) for b in range(4) for c in range(2) if (a, b, c) != (0, 0, 0)]
ORDER = [29, 12, 4, 23, 17, 8, 26, 1, 14, 20, 6, 30, 10, 3, 25, 16, 22, 9, 0, 27, 13, 18, 5, 24, 11, 2, 28, 19, 7, 15, 21]


def shifted(gy, offset):
    dz, dy, dc = offset
    z, y, c = gy // 8, (gy // 2) % 4, gy % 2
    return (((z + dz) % 4) * 4 + (y + dy) % 4) * 2 + (c + dc) % 2


def split(x, pieces):
    out = []
    for _ in range(pieces - 1):
        hi = x.astype(BF16)
        out.append(hi)
        x = x - hi.astype(F32)
    out.append(x.astype(BF16))
    return out


def dot(a, b, dims):
    return lax.dot_general(a, b, dims, preferred_element_type=F32)


def pick(x, onehot, dims=NN):
    parts = [dot(p, onehot, dims) for p in split(x, 3)]
    return parts[0] + (parts[1] + parts[2])


def pick_rows(onehot, x, dims=NN):
    parts = [dot(onehot, p, dims) for p in split(x, 3)]
    return parts[0] + (parts[1] + parts[2])


def iota(shape, dim):
    return lax.broadcasted_iota(jnp.int32, shape, dim)


def hot(cond):
    return jnp.where(cond, 1.0, 0.0).astype(BF16)


def padded(s):
    if s.shape[0] == PAD:
        return s
    return jnp.concatenate([s, jnp.zeros((PAD - LEV, s.shape[1]), F32)], axis=0)


def step_kernel(
    slot_ref, source_ref, gcm_ref, crm_hbm,
    out_ref, tend_ref,
    crm, gpad, x1s, x1r, x2s, x2r, r1s, r1r, r2s, r2r, spread, spread_of, fin, warm, send, mean_sc, coef,
    crm_sem, own_sem, s1, v1, s2, v2, s3, v3, s4, v4, s5, v5,
):
    gx = lax.axis_index("gx")
    gy = lax.axis_index("gy")
    peers_x = [(gx + d) % NX for d in (1, 2, 3)]
    peers_y = [shifted(gy, OFFSETS[i]) for i in ORDER]

    barrier = pltpu.get_barrier_semaphore()
    for tx in peers_x:
        pl.semaphore_signal(barrier, inc=1, device_id={"gx": tx}, device_id_type=MESH)
    for ty in peers_y:
        pl.semaphore_signal(barrier, inc=1, device_id={"gy": ty}, device_id_type=MESH)

    load = pltpu.make_async_copy(crm_hbm, crm, crm_sem)
    load.start()

    gpad[...] = jnp.zeros((4, PAD, LANES), F32)
    gpad[0:3, 0:LEV, :] = gcm_ref[...]
    source = source_ref[...]
    chosen = hot(iota((LANES, LANES), 0) == source)
    packed = pick(gpad[...].reshape(4 * PAD, LANES), chosen)
    x1s[0] = packed[0:128].T
    x1s[1] = packed[128:256].T

    pl.semaphore_wait(barrier, 3 + 31)

    own_rows = pl.ds(pl.multiple_of(gx * 32, 32), 32)
    stage1 = []
    for i, tx in enumerate(peers_x):
        copy = pltpu.make_async_remote_copy(
            src_ref=x1s.at[:, pl.ds(pl.multiple_of(tx * 32, 32), 32), :],
            dst_ref=x1r.at[:, own_rows, :],
            send_sem=s1.at[i], recv_sem=v1.at[i], device_id={"gx": tx}, device_id_type=MESH,
        )
        copy.start()
        stage1.append(copy)
    x1r[:, own_rows, :] = x1s[:, own_rows, :]

    def fill(g, carry):
        cols = g * 4 + iota((LANES, LANES), 1) // CRM_X
        spread_of[:, pl.ds(pl.multiple_of(g * LANES, LANES), LANES)] = hot(iota((LANES, LANES), 0) == cols)
        return carry
    lax.fori_loop(0, GROUPS, fill, 0)

    for copy in stage1:
        copy.wait()
    row = iota((256, LANES), 0)
    col = iota((256, LANES), 1)
    here = (row // 8 == col % 32)
    perm = [hot(here & (row % 8 == (col // 32) * 2 + h)) for h in range(2)]
    x2s[...] = (pick_rows(perm[0], x1r[0]) + pick_rows(perm[1], x1r[1])).reshape(32, 8, LANES)
    stage2 = []
    for i, ty in enumerate(peers_y):
        copy = pltpu.make_async_remote_copy(
            src_ref=x2s.at[ty], dst_ref=x2r.at[gy],
            send_sem=s2.at[i], recv_sem=v2.at[i], device_id={"gy": ty}, device_id_type=MESH,
        )
        copy.start()
        stage2.append(copy)
    x2r[gy] = x2s[gy]

    load.wait()

    def column_means(ref_a, ref_b, out_ref):
        out_ref[...] = jnp.zeros((2 * PAD, LANES), F32)

        def add(i, carry):
            lanes = pl.ds(pl.multiple_of(i * 512, 512), 512)
            both = jnp.concatenate([padded(ref_a[:, lanes]), padded(ref_b[:, lanes])], axis=0)
            hi, lo = split(both, 2)
            e = spread_of[:, lanes]
            out_ref[...] += dot(hi, e, NT) + dot(lo, e, NT)
            return carry
        lax.fori_loop(0, 8, add, 0)
        return out_ref[...] * (1.0 / CRM_X)

    level = iota((PAD, LANES), 0)
    means = column_means(crm.at[0], crm.at[1], mean_sc)

    def below(s):
        return jnp.where(level == 0, s, pltpu.roll(s, 1, 0))

    def above(s):
        return jnp.where(level == LEV - 1, s, pltpu.roll(s, PAD - 1, 0))

    moved_mean = []
    for f in range(2):
        m = means[f * PAD:(f + 1) * PAD]
        moved_mean.append(0.8 * m + 0.1 * (below(m) + above(m)))

    for copy in stage2:
        copy.wait()
    landed = x2r[...].reshape(256, LANES).T
    first = pick(landed, perm[0])
    wind = pick(landed[0:PAD], perm[1])
    target = [first[0:PAD], first[PAD:128]]
    columns = jnp.concatenate(
        [0.125 * jnp.tanh(wind)] + [0.5 * (target[f] - moved_mean[f]) for f in range(2)], axis=0)
    hi, lo = split(columns, 2)
    coef[0] = hi
    coef[1] = lo

    def spread_out(i, carry):
        lanes = pl.ds(pl.multiple_of(i * 512, 512), 512)
        e = spread_of[:, lanes]
        spread[:, lanes] = dot(coef[0], e, NN) + dot(coef[1], e, NN)
        return carry
    lax.fori_loop(0, 8, spread_out, 0)

    x = iota((PAD, LANES), 1) % CRM_X

    def advance(s, speed, shift):
        west = jnp.where(x == 0, pltpu.roll(s, LANES - 31, 1), pltpu.roll(s, 1, 1))
        east = jnp.where(x == CRM_X - 1, pltpu.roll(s, 31, 1), pltpu.roll(s, LANES - 1, 1))
        return (0.6 * s + 0.1 * ((east + west) + (below(s) + above(s))) - speed * (east - west)) + shift

    def one_group(g, carry):
        lanes = pl.ds(pl.multiple_of(g * LANES, LANES), LANES)
        speed = spread[0:PAD, lanes]
        energy = advance(padded(crm[0, :, lanes]), speed, spread[PAD:2 * PAD, lanes])
        water = advance(padded(crm[1, :, lanes]), speed, spread[2 * PAD:3 * PAD, lanes])
        base = 0.5 * energy + (1.25 * water - 0.625)
        half = base - 0.625 * jnp.tanh(0.5 * energy)
        half = base - 0.625 * jnp.tanh(half)
        half = base - 0.625 * jnp.tanh(half)
        final = 0.8 * water + (0.1 + 0.1 * jnp.tanh(half))
        warm[0, :, lanes] = half + half
        warm[1, :, lanes] = final
        fin[g, 0] = energy[0:LEV]
        fin[g, 1] = final[0:LEV]
        return carry
    lax.fori_loop(0, GROUPS, one_group, 0)

    ends = column_means(warm.at[0], warm.at[1], mean_sc)
    tendency = ends - first
    back = hot((row // 8 == col % 32) & (row % 8 == col // 32))
    r1s[...] = pick_rows(back, tendency, NT).reshape(32, 8, LANES)
    stage3 = []
    for i, ty in enumerate(peers_y):
        copy = pltpu.make_async_remote_copy(
            src_ref=r1s.at[ty], dst_ref=r1r.at[gy],
            send_sem=s3.at[i], recv_sem=v3.at[i], device_id={"gy": ty}, device_id_type=MESH,
        )
        copy.start()
        stage3.append(copy)
    r1r[gy] = r1s[gy]

    def gather(i, d):
        for r in range(2):
            g = slot_ref[d * 2 + r]
            block = fin[jnp.maximum(g, 0)]
            send[i, :, :, r * LANES:(r + 1) * LANES] = jnp.where(g >= 0, block, 0.0)

    own_lanes = pl.ds(pl.multiple_of(gy * 256, 256), 256)
    moves = []
    for i, ty in enumerate(peers_y):
        gather(i, ty)
        copy = pltpu.make_async_remote_copy(
            src_ref=send.at[i], dst_ref=out_ref.at[:, :, own_lanes],
            send_sem=s5.at[i], recv_sem=v5.at[i], device_id={"gy": ty}, device_id_type=MESH,
        )
        copy.start()
        moves.append(copy)
    gather(31, gy)
    own = pltpu.make_async_copy(send.at[31], out_ref.at[:, :, own_lanes], own_sem)
    own.start()

    for copy in stage3:
        copy.wait()
    rows = iota((LANES, 256), 0)
    cols = iota((LANES, 256), 1)
    r2s[...] = pick_rows(hot((rows % 32 == cols // 8) & (rows // 32 == cols % 8)), r1r[...].reshape(256, LANES))
    stage4 = []
    for i, tx in enumerate(peers_x):
        copy = pltpu.make_async_remote_copy(
            src_ref=r2s.at[pl.ds(pl.multiple_of(tx * 32, 32), 32), :], dst_ref=r2r.at[own_rows, :],
            send_sem=s4.at[i], recv_sem=v4.at[i], device_id={"gx": tx}, device_id_type=MESH,
        )
        copy.start()
        stage4.append(copy)
    r2r[own_rows, :] = r2s[own_rows, :]
    for copy in stage4:
        copy.wait()
    placed = pick(r2r[...].T, chosen, NT)
    tend_ref[0] = placed[0:LEV]
    tend_ref[1] = placed[PAD:PAD + LEV]

    own.wait()
    for copy in moves:
        copy.wait()


def slots_of(group_owner):
    g = jnp.arange(GROUPS, dtype=jnp.int32)[None, :]
    same = group_owner[None, :] == jnp.arange(NY, dtype=jnp.int32)[:, None]
    low = jnp.min(jnp.where(same, g, GROUPS), axis=1)
    high = jnp.max(jnp.where(same, g, -1), axis=1)
    return jnp.stack([jnp.where(high < 0, -1, low), jnp.where(high > low, high, -1)], axis=1).reshape(2 * NY)


def on_device(gcm_state, crm_state, send_source, group_owner):
    vm = pltpu.VMEM
    dma = pltpu.SemaphoreType.DMA
    crm_next, tendency = pl.pallas_call(
        step_kernel,
        out_shape=(jax.ShapeDtypeStruct((2, LEV, 8192), F32), jax.ShapeDtypeStruct((2, LEV, LANES), F32)),
        in_specs=[
            pl.BlockSpec(memory_space=pltpu.SMEM),
            pl.BlockSpec(memory_space=pltpu.VMEM),
            pl.BlockSpec(memory_space=pltpu.VMEM),
            pl.BlockSpec(memory_space=pl.ANY),
        ],
        out_specs=(pl.BlockSpec(memory_space=pl.ANY), pl.BlockSpec(memory_space=pltpu.VMEM)),
        scratch_shapes=[
            vm((2, LEV, 4096), F32), vm((4, PAD, LANES), F32),
            vm((2, 128, LANES), F32), vm((2, 128, LANES), F32),
            vm((32, 8, LANES), F32), vm((32, 8, LANES), F32),
            vm((32, 8, LANES), F32), vm((32, 8, LANES), F32),
            vm((128, LANES), F32), vm((128, LANES), F32),
            vm((3 * PAD, 4096), F32), vm((LANES, 4096), BF16),
            vm((GROUPS, 2, LEV, LANES), F32), vm((2, PAD, 4096), F32),
            vm((32, 2, LEV, 256), F32), vm((2 * PAD, LANES), F32), vm((2, 3 * PAD, LANES), BF16),
            dma, dma, dma((3,)), dma((3,)), dma((31,)), dma((31,)), dma((31,)), dma((31,)),
            dma((3,)), dma((3,)), dma((31,)), dma((31,)),
        ],
        compiler_params=pltpu.CompilerParams(collective_id=0, has_side_effects=True, vmem_limit_bytes=48 << 20),
    )(slots_of(group_owner), send_source.reshape(1, LANES), gcm_state, crm_state)
    return tendency, crm_next


def solution(mesh):
    spec = P(None, None, ("gx", "gy"))
    flat = P(("gx", "gy"))
    return jax.shard_map(
        on_device, mesh=mesh, in_specs=(spec, spec, flat, flat), out_specs=(spec, spec), check_vma=False)
```

```python
import functools

import jax
import jax.numpy as jnp
from jax import lax
from jax.experimental import pallas as pl
from jax.experimental.pallas import tpu as pltpu
from jax.sharding import PartitionSpec as P

CRM_X = 32
LEV = 58
PAD = 64
LANES = 128
NX = 4
NY = 32
GROUPS = 32
GROUP = 4
F32 = jnp.float32
BF16 = jnp.bfloat16
MESH = pl.DeviceIdType.MESH

NN = (((1,), (0,)), ((), ()))
NT = (((1,), (1,)), ((), ()))

RAW = 16
WAVES = (3, 10, RAW)
STRIDE = 13


def peer(gy, i, sign):
    offset = (STRIDE * (i + 1)) % NY
    z = (gy // 8 + 4 + sign * (offset // 8)) % 4
    y = ((gy // 2) % 4 + 4 + sign * ((offset // 2) % 4)) % 4
    return (z * 4 + y) * 2 + (gy + offset) % 2


def split(x, pieces):
    out = []
    for _ in range(pieces - 1):
        hi = x.astype(BF16)
        out.append(hi)
        x = x - hi.astype(F32)
    out.append(x.astype(BF16))
    return out


def dot(a, b, dims):
    return lax.dot_general(a, b, dims, preferred_element_type=F32)


def pick(x, onehot, dims=NN):
    parts = [dot(p, onehot, dims) for p in split(x, 3)]
    return parts[0] + (parts[1] + parts[2])


def pick_rows(onehot, x, dims=NN):
    parts = [dot(onehot, p, dims) for p in split(x, 3)]
    return parts[0] + (parts[1] + parts[2])


def iota(shape, dim):
    return lax.broadcasted_iota(jnp.int32, shape, dim)


def hot(cond):
    return jnp.where(cond, 1.0, 0.0).astype(BF16)


def padded(s):
    if s.shape[0] == PAD:
        return s
    return jnp.concatenate([s, jnp.zeros((PAD - LEV, s.shape[1]), F32)], axis=0)


def step_kernel(
    slot_ref, lane_ref, source_hbm, gcm_hbm, crm_hbm,
    out_ref, tend_ref,
    crm, groups, gcm, source_of, gpad, x1s, x1r, x2s, x2r, r1s, r1r, r2s, r2r, spread, spread_of, fin, warm, send, mean_sc, coef, c6s, c6r,
    crm_sem, gcm_sem, source_sem, own_sem, s1, v1, s2, v2, s3, v3, s4, v4, s5, v5, s6, v6,
):
    gx = lax.axis_index("gx")
    gy = lax.axis_index("gy")
    peers_x = [(gx + d) % NX for d in (1, 2, 3)]
    peers_y = [peer(gy, i, 1) for i in range(NY - 1)]
    gcm_load = pltpu.make_async_copy(gcm_hbm, gcm, gcm_sem)
    gcm_load.start()
    source_load = pltpu.make_async_copy(source_hbm, source_of, source_sem)
    source_load.start()
    load = pltpu.make_async_copy(crm_hbm, crm, crm_sem)
    load.start()

    barrier = pltpu.get_barrier_semaphore()
    for tx in peers_x:
        pl.semaphore_signal(barrier, inc=1, device_id={"gx": tx}, device_id_type=MESH)
    for ty in peers_y:
        pl.semaphore_signal(barrier, inc=1, device_id={"gy": ty}, device_id_type=MESH)

    gpad[...] = jnp.zeros((4, PAD, LANES), F32)
    gcm_load.wait()
    source_load.wait()
    gpad[0:3, 0:LEV, :] = gcm[...]
    source = source_of[...]
    chosen = hot(iota((LANES, LANES), 0) == source)
    packed = pick(gpad[...].reshape(4 * PAD, LANES), chosen)
    x1s[0] = packed[0:128].T
    x1s[1] = packed[128:256].T

    pl.semaphore_wait(barrier, 3 + 31)

    own_rows = pl.ds(pl.multiple_of(gx * 32, 32), 32)
    stage1 = []
    for i, tx in enumerate(peers_x):
        copy = pltpu.make_async_remote_copy(
            src_ref=x1s.at[:, pl.ds(pl.multiple_of(tx * 32, 32), 32), :],
            dst_ref=x1r.at[:, own_rows, :],
            send_sem=s1.at[i], recv_sem=v1.at[i], device_id={"gx": tx}, device_id_type=MESH,
        )
        copy.start()
        stage1.append(copy)
    x1r[:, own_rows, :] = x1s[:, own_rows, :]

    own_lanes = pl.ds(pl.multiple_of(gy * 256, 256), 256)

    def state_copy(i):
        return pltpu.make_async_remote_copy(
            src_ref=send.at[i], dst_ref=out_ref.at[:, :, own_lanes],
            send_sem=s5.at[i], recv_sem=v5.at[i], device_id={"gy": peer(gy, i, 1)}, device_id_type=MESH,
        )

    def coef_copy(i):
        return pltpu.make_async_remote_copy(
            src_ref=c6s.at[peer(gy, i, 1)], dst_ref=c6r.at[i],
            send_sem=s6.at[i], recv_sem=v6.at[i], device_id={"gy": peer(gy, i, 1)}, device_id_type=MESH,
        )

    def send_raw(i, carry):
        d = peer(gy, i, 1)
        for r in range(2):
            g = slot_ref[d * 2 + r]
            block = groups[jnp.maximum(g, 0)]
            block = jnp.where(g >= 0, block, 0.0)
            for f in range(2):
                send[i, :, f, r * LANES:(r + 1) * LANES] = block[f]
        state_copy(i).start()
        return carry

    load.wait()

    def by_group(g, carry):
        lanes = pl.ds(pl.multiple_of(g * LANES, LANES), LANES)
        for f in range(2):
            groups[g, f] = crm[:, f, lanes]
        return carry
    lax.fori_loop(0, GROUPS, by_group, 0)
    lax.fori_loop(0, WAVES[0], send_raw, 0)

    def fill(g, carry):
        cols = g * 4 + iota((LANES, LANES), 1) // CRM_X
        spread_of[:, pl.ds(pl.multiple_of(g * LANES, LANES), LANES)] = hot(iota((LANES, LANES), 0) == cols)
        return carry
    lax.fori_loop(0, GROUPS, fill, 0)

    for copy in stage1:
        copy.wait()
    row = iota((256, LANES), 0)
    col = iota((256, LANES), 1)
    here = (row // 8 == col % 32)
    perm = [hot(here & (row % 8 == (col // 32) * 2 + h)) for h in range(2)]
    x2s[...] = (pick_rows(perm[0], x1r[0]) + pick_rows(perm[1], x1r[1])).reshape(32, 8, LANES)
    stage2 = []
    for i, ty in enumerate(peers_y):
        copy = pltpu.make_async_remote_copy(
            src_ref=x2s.at[ty], dst_ref=x2r.at[gy],
            send_sem=s2.at[i], recv_sem=v2.at[i], device_id={"gy": ty}, device_id_type=MESH,
        )
        copy.start()
        stage2.append(copy)
    x2r[gy] = x2s[gy]

    lax.fori_loop(WAVES[0], WAVES[1], send_raw, 0)


    def column_means(read, out_ref):
        out_ref[...] = jnp.zeros((2 * PAD, LANES), F32)

        def add(i, carry):
            lanes = pl.ds(pl.multiple_of(i * 512, 512), 512)
            both = jnp.concatenate([padded(read(0, lanes)), padded(read(1, lanes))], axis=0)
            hi, lo = split(both, 2)
            e = spread_of[:, lanes]
            out_ref[...] += dot(hi, e, NT) + dot(lo, e, NT)
            return carry
        lax.fori_loop(0, 8, add, 0)
        return out_ref[...] * (1.0 / CRM_X)

    level = iota((PAD, LANES), 0)
    means = column_means(lambda f, lanes: crm[:, f, lanes], mean_sc)

    def below(s):
        return jnp.where(level == 0, s, pltpu.roll(s, 1, 0))

    def above(s):
        return jnp.where(level == LEV - 1, s, pltpu.roll(s, PAD - 1, 0))

    moved_mean = []
    for f in range(2):
        m = means[f * PAD:(f + 1) * PAD]
        moved_mean.append(0.8 * m + 0.1 * (below(m) + above(m)))

    for copy in stage2:
        copy.wait()
    landed = x2r[...].reshape(256, LANES).T
    first = pick(landed, perm[0])
    wind = pick(landed[0:PAD], perm[1])
    target = [first[0:PAD], first[PAD:128]]
    columns = jnp.concatenate(
        [0.125 * jnp.tanh(wind)] + [0.5 * (target[f] - moved_mean[f]) for f in range(2)]
        + [jnp.ones((PAD, LANES), F32)], axis=0)
    hi, lo = split(columns, 2)
    coef[0] = hi
    coef[1] = lo
    to_slot = hot(iota((LANES, 256), 0) == lane_ref[...])
    c6s[...] = pick(columns, to_slot).T.reshape(NY, 8, 256)

    def send_coef(i, carry):
        coef_copy(i).start()
        return carry
    lax.fori_loop(0, RAW, send_coef, 0)
    lax.fori_loop(WAVES[1], WAVES[2], send_raw, 0)

    def spread_out(i, carry):
        lanes = pl.ds(pl.multiple_of(i * 512, 512), 512)
        e = spread_of[:, lanes]
        spread[:, lanes] = dot(coef[0, 0:3 * PAD], e, NN) + dot(coef[1, 0:3 * PAD], e, NN)
        return carry
    lax.fori_loop(0, 8, spread_out, 0)

    x = iota((PAD, LANES), 1) % CRM_X

    def advance(s, speed, shift):
        west = jnp.where(x == 0, pltpu.roll(s, LANES - 31, 1), pltpu.roll(s, 1, 1))
        east = jnp.where(x == CRM_X - 1, pltpu.roll(s, 31, 1), pltpu.roll(s, LANES - 1, 1))
        return (0.6 * s + 0.1 * ((east + west) + (below(s) + above(s))) - speed * (east - west)) + shift

    def physics(s0, s1, speed, shift0, shift1):
        energy = advance(padded(s0), speed, shift0)
        water = advance(padded(s1), speed, shift1)
        base = 0.5 * energy + (1.25 * water - 0.625)
        half = base - 0.625 * jnp.tanh(0.5 * energy)
        half = base - 0.625 * jnp.tanh(half)
        half = base - 0.625 * jnp.tanh(half)
        return energy, 0.8 * water + (0.1 + 0.1 * jnp.tanh(half)), half

    def one_group(g, carry):
        lanes = pl.ds(pl.multiple_of(g * LANES, LANES), LANES)
        energy, final, half = physics(
            groups[g, 0], groups[g, 1],
            spread[0:PAD, lanes], spread[PAD:2 * PAD, lanes], spread[2 * PAD:3 * PAD, lanes])
        warm[0, :, lanes] = half + half
        warm[1, :, lanes] = final
        fin[g, 0] = energy[0:LEV]
        fin[g, 1] = final[0:LEV]
        return carry
    lax.fori_loop(0, GROUPS, one_group, 0)

    ends = column_means(lambda f, lanes: warm[f, :, lanes], mean_sc)
    tendency = ends - first
    back = hot((row // 8 == col % 32) & (row % 8 == col // 32))
    r1s[...] = pick_rows(back, tendency, NT).reshape(32, 8, LANES)
    stage3 = []
    for i, ty in enumerate(peers_y):
        copy = pltpu.make_async_remote_copy(
            src_ref=r1s.at[ty], dst_ref=r1r.at[gy],
            send_sem=s3.at[i], recv_sem=v3.at[i], device_id={"gy": ty}, device_id_type=MESH,
        )
        copy.start()
        stage3.append(copy)
    r1r[gy] = r1s[gy]

    def gather(i, d):
        for r in range(2):
            g = slot_ref[d * 2 + r]
            block = fin[jnp.maximum(g, 0)]
            block = jnp.where(g >= 0, block, 0.0)
            for f in range(2):
                send[i, :, f, r * LANES:(r + 1) * LANES] = block[f]

    def send_final(i, carry):
        gather(i, peer(gy, i, 1))
        state_copy(i).start()
        return carry
    lax.fori_loop(RAW, NY - 1, send_final, 0)
    gather(31, gy)
    own = pltpu.make_async_copy(send.at[31], out_ref.at[:, :, own_lanes], own_sem)
    own.start()

    def wait_coef(i, carry):
        coef_copy(i).wait()
        return carry
    lax.fori_loop(0, RAW, wait_coef, 0)
    came = split(c6r[...].reshape(RAW * 8, 256).T, 2)

    def finish(i, carry):
        state_copy(i).wait()
        e = hot(iota((RAW * 8, 256), 0) == i * 8 + iota((RAW * 8, 256), 1) // CRM_X)
        both = dot(came[0], e, NN) + dot(came[1], e, NN)
        start = peer(gy, i, -1) * 256
        for r in range(2):
            c = both[:, r * LANES:(r + 1) * LANES]
            lanes = pl.ds(pl.multiple_of(start + r * LANES, LANES), LANES)
            energy, final, _ = physics(
                out_ref[:, 0, lanes], out_ref[:, 1, lanes], c[0:PAD], c[PAD:2 * PAD], c[2 * PAD:3 * PAD])
            out_ref[:, 0, lanes] = energy[0:LEV]
            out_ref[:, 1, lanes] = (c[3 * PAD:] * final)[0:LEV]
        return carry
    lax.fori_loop(0, RAW, finish, 0)

    for copy in stage3:
        copy.wait()
    rows = iota((LANES, 256), 0)
    cols = iota((LANES, 256), 1)
    r2s[...] = pick_rows(hot((rows % 32 == cols // 8) & (rows // 32 == cols % 8)), r1r[...].reshape(256, LANES))
    stage4 = []
    for i, tx in enumerate(peers_x):
        copy = pltpu.make_async_remote_copy(
            src_ref=r2s.at[pl.ds(pl.multiple_of(tx * 32, 32), 32), :], dst_ref=r2r.at[own_rows, :],
            send_sem=s4.at[i], recv_sem=v4.at[i], device_id={"gx": tx}, device_id_type=MESH,
        )
        copy.start()
        stage4.append(copy)
    r2r[own_rows, :] = r2s[own_rows, :]
    for copy in stage4:
        copy.wait()
    placed = pick(r2r[...].T, chosen, NT)
    tend_ref[:, 0, :] = placed[0:LEV]
    tend_ref[:, 1, :] = placed[PAD:PAD + LEV]

    own.wait()

    def wait_final(i, carry):
        state_copy(i).wait()
        return carry
    lax.fori_loop(RAW, NY - 1, wait_final, 0)


def slots_of(group_owner):
    g = jnp.arange(GROUPS, dtype=jnp.int32)[None, :]
    same = group_owner[None, :] == jnp.arange(NY, dtype=jnp.int32)[:, None]
    low = jnp.min(jnp.where(same, g, GROUPS), axis=1)
    high = jnp.max(jnp.where(same, g, -1), axis=1)
    return jnp.stack([jnp.where(high < 0, -1, low), jnp.where(high > low, high, -1)], axis=1).reshape(2 * NY)


def on_device(gcm_state, crm_state, send_source, group_owner):
    vm = pltpu.VMEM
    dma = pltpu.SemaphoreType.DMA
    slots = slots_of(group_owner)
    lane = (slots[:, None] * GROUP + jnp.arange(GROUP, dtype=jnp.int32)[None, :]).reshape(1, 256)
    hbm = pl.BlockSpec(memory_space=pltpu.HBM)
    vmem = pl.BlockSpec(memory_space=pltpu.VMEM)
    crm_next, tendency = pl.pallas_call(
        step_kernel,
        out_shape=(jax.ShapeDtypeStruct((LEV, 2, 8192), F32), jax.ShapeDtypeStruct((LEV, 2, LANES), F32)),
        in_specs=[pl.BlockSpec(memory_space=pltpu.SMEM), vmem, hbm, hbm, hbm],
        out_specs=(vmem, vmem),
        scratch_shapes=[
            vm((LEV, 2, 4096), F32), vm((GROUPS, 2, LEV, LANES), F32), vm((3, LEV, LANES), F32), vm((1, LANES), jnp.int32), vm((4, PAD, LANES), F32),
            vm((2, 128, LANES), F32), vm((2, 128, LANES), F32),
            vm((32, 8, LANES), F32), vm((32, 8, LANES), F32),
            vm((32, 8, LANES), F32), vm((32, 8, LANES), F32),
            vm((128, LANES), F32), vm((128, LANES), F32),
            vm((3 * PAD, 4096), F32), vm((LANES, 4096), BF16),
            vm((GROUPS, 2, LEV, LANES), F32), vm((2, PAD, 4096), F32),
            vm((32, LEV, 2, 256), F32), vm((2 * PAD, LANES), F32), vm((2, 4 * PAD, LANES), BF16),
            vm((NY, 8, 256), F32), vm((RAW, 8, 256), F32),
            dma, dma, dma, dma, dma((3,)), dma((3,)), dma((31,)), dma((31,)), dma((31,)), dma((31,)),
            dma((3,)), dma((3,)), dma((31,)), dma((31,)), dma((RAW,)), dma((RAW,)),
        ],
        compiler_params=pltpu.CompilerParams(collective_id=0, has_side_effects=True, vmem_limit_bytes=48 << 20),
    )(slots, lane, send_source.reshape(1, LANES), gcm_state, crm_state.transpose(1, 0, 2))
    return tendency.transpose(1, 0, 2), crm_next.transpose(1, 0, 2)


def solution(mesh):
    spec = P(None, None, ("gx", "gy"))
    flat = P(("gx", "gy"))
    return jax.shard_map(
        on_device, mesh=mesh, in_specs=(spec, spec, flat, flat), out_specs=(spec, spec), check_vma=False)
```

```python
import functools

import jax
import jax.numpy as jnp
from jax import lax
from jax.experimental import pallas as pl
from jax.experimental.pallas import tpu as pltpu
from jax.sharding import PartitionSpec as P

CRM_X = 32
LEV = 58
PAD = 64
LANES = 128
NX = 4
NY = 32
GROUPS = 32
GROUP = 4
F32 = jnp.float32
BF16 = jnp.bfloat16
MESH = pl.DeviceIdType.MESH

NN = (((1,), (0,)), ((), ()))
NT = (((1,), (1,)), ((), ()))

RAW = 16
WAVES = (4, 10, RAW)
STRIDE = 13


def peer(gy, i, sign):
    offset = (STRIDE * (i + 1)) % NY
    z = (gy // 8 + 4 + sign * (offset // 8)) % 4
    y = ((gy // 2) % 4 + 4 + sign * ((offset // 2) % 4)) % 4
    return (z * 4 + y) * 2 + (gy + offset) % 2


def split(x, pieces):
    out = []
    for _ in range(pieces - 1):
        hi = x.astype(BF16)
        out.append(hi)
        x = x - hi.astype(F32)
    out.append(x.astype(BF16))
    return out


def dot(a, b, dims):
    return lax.dot_general(a, b, dims, preferred_element_type=F32)


def pick(x, onehot, dims=NN):
    parts = [dot(p, onehot, dims) for p in split(x, 3)]
    return parts[0] + (parts[1] + parts[2])


def pick_rows(onehot, x, dims=NN):
    parts = [dot(onehot, p, dims) for p in split(x, 3)]
    return parts[0] + (parts[1] + parts[2])


def iota(shape, dim):
    return lax.broadcasted_iota(jnp.int32, shape, dim)


def hot(cond):
    return jnp.where(cond, 1.0, 0.0).astype(BF16)


def padded(s):
    if s.shape[0] == PAD:
        return s
    return jnp.concatenate([s, jnp.zeros((PAD - LEV, s.shape[1]), F32)], axis=0)


def step_kernel(
    owner_hbm, source_hbm, gcm_hbm, crm_hbm,
    out_ref, tend_ref,
    crm, groups, gcm, source_of, gpad, x1s, x1r, x2s, x2r, r1s, r1r, r2s, r2r, spread, spread_of, fin, warm, send, mean_sc, coef, c6s, c6r, coef_rows,
    owner, crm_sem, owner_sem, gcm_sem, source_sem, own_sem, s1, v1, s2, v2, s3, v3, s4, v4, s5, v5, s6, v6,
):
    gx = lax.axis_index("gx")
    gy = lax.axis_index("gy")
    peers_x = [(gx + d) % NX for d in (1, 2, 3)]
    peers_y = [peer(gy, i, 1) for i in range(NY - 1)]
    owner_load = pltpu.make_async_copy(owner_hbm, owner, owner_sem)
    owner_load.start()
    gcm_load = pltpu.make_async_copy(gcm_hbm, gcm, gcm_sem)
    gcm_load.start()
    source_load = pltpu.make_async_copy(source_hbm, source_of, source_sem)
    source_load.start()
    load = pltpu.make_async_copy(crm_hbm, crm, crm_sem)
    load.start()

    barrier = pltpu.get_barrier_semaphore()
    for tx in peers_x:
        pl.semaphore_signal(barrier, inc=1, device_id={"gx": tx}, device_id_type=MESH)
    for ty in peers_y:
        pl.semaphore_signal(barrier, inc=1, device_id={"gy": ty}, device_id_type=MESH)

    own_lanes = pl.ds(pl.multiple_of(gy * 256, 256), 256)

    def state_copy(i):
        return pltpu.make_async_remote_copy(
            src_ref=send.at[i], dst_ref=out_ref.at[:, :, own_lanes],
            send_sem=s5.at[i], recv_sem=v5.at[i], device_id={"gy": peer(gy, i, 1)}, device_id_type=MESH,
        )

    def coef_copy(i):
        return pltpu.make_async_remote_copy(
            src_ref=c6s.at[i], dst_ref=c6r.at[i],
            send_sem=s6.at[i], recv_sem=v6.at[i], device_id={"gy": peer(gy, i, 1)}, device_id_type=MESH,
        )

    def slots_for(d):
        low, high = jnp.int32(GROUPS), jnp.int32(-1)
        for g in range(GROUPS):
            same = owner[g] == d
            low = jnp.minimum(low, jnp.where(same, g, GROUPS))
            high = jnp.where(same, g, high)
        return jnp.where(high < 0, -1, low), jnp.where(high > low, high, -1)

    def gather(i, d, blocks):
        for r, g in enumerate(slots_for(d)):
            block = blocks[jnp.maximum(g, 0)]
            block = jnp.where(g >= 0, block, 0.0)
            for f in range(2):
                send[i, :, f, r * LANES:(r + 1) * LANES] = block[f]

    def send_raw(i, carry):
        gather(i, peer(gy, i, 1), groups)
        state_copy(i).start()
        return carry

    load.wait()
    owner_load.wait()

    def by_group(g, carry):
        lanes = pl.ds(pl.multiple_of(g * LANES, LANES), LANES)
        for f in range(2):
            groups[g, f] = crm[:, f, lanes]
        return carry
    lax.fori_loop(0, GROUPS, by_group, 0)
    pl.semaphore_wait(barrier, 3 + 31)
    lax.fori_loop(0, WAVES[0], send_raw, 0)

    gpad[...] = jnp.zeros((4, PAD, LANES), F32)
    gcm_load.wait()
    source_load.wait()
    gpad[0:3, 0:LEV, :] = gcm[...]
    source = source_of[...]
    chosen = hot(iota((LANES, LANES), 0) == source)
    packed = pick(gpad[...].reshape(4 * PAD, LANES), chosen)
    x1s[0] = packed[0:128].T
    x1s[1] = packed[128:256].T

    own_rows = pl.ds(pl.multiple_of(gx * 32, 32), 32)
    stage1 = []
    for i, tx in enumerate(peers_x):
        copy = pltpu.make_async_remote_copy(
            src_ref=x1s.at[:, pl.ds(pl.multiple_of(tx * 32, 32), 32), :],
            dst_ref=x1r.at[:, own_rows, :],
            send_sem=s1.at[i], recv_sem=v1.at[i], device_id={"gx": tx}, device_id_type=MESH,
        )
        copy.start()
        stage1.append(copy)
    x1r[:, own_rows, :] = x1s[:, own_rows, :]


    def fill(g, carry):
        cols = g * 4 + iota((LANES, LANES), 1) // CRM_X
        spread_of[:, pl.ds(pl.multiple_of(g * LANES, LANES), LANES)] = hot(iota((LANES, LANES), 0) == cols)
        return carry
    lax.fori_loop(0, GROUPS, fill, 0)

    for copy in stage1:
        copy.wait()
    row = iota((256, LANES), 0)
    col = iota((256, LANES), 1)
    here = (row // 8 == col % 32)
    perm = [hot(here & (row % 8 == (col // 32) * 2 + h)) for h in range(2)]
    x2s[...] = (pick_rows(perm[0], x1r[0]) + pick_rows(perm[1], x1r[1])).reshape(32, 8, LANES)
    stage2 = []
    for i, ty in enumerate(peers_y):
        copy = pltpu.make_async_remote_copy(
            src_ref=x2s.at[ty], dst_ref=x2r.at[gy],
            send_sem=s2.at[i], recv_sem=v2.at[i], device_id={"gy": ty}, device_id_type=MESH,
        )
        copy.start()
        stage2.append(copy)
    x2r[gy] = x2s[gy]

    lax.fori_loop(WAVES[0], WAVES[1], send_raw, 0)


    def column_means(read, out_ref):
        out_ref[...] = jnp.zeros((2 * PAD, LANES), F32)

        def add(i, carry):
            lanes = pl.ds(pl.multiple_of(i * 512, 512), 512)
            both = jnp.concatenate([padded(read(0, lanes)), padded(read(1, lanes))], axis=0)
            hi, lo = split(both, 2)
            e = spread_of[:, lanes]
            out_ref[...] += dot(hi, e, NT) + dot(lo, e, NT)
            return carry
        lax.fori_loop(0, 8, add, 0)
        return out_ref[...] * (1.0 / CRM_X)

    level = iota((PAD, LANES), 0)
    means = column_means(lambda f, lanes: crm[:, f, lanes], mean_sc)

    def below(s):
        return jnp.where(level == 0, s, pltpu.roll(s, 1, 0))

    def above(s):
        return jnp.where(level == LEV - 1, s, pltpu.roll(s, PAD - 1, 0))

    moved_mean = []
    for f in range(2):
        m = means[f * PAD:(f + 1) * PAD]
        moved_mean.append(0.8 * m + 0.1 * (below(m) + above(m)))

    for copy in stage2:
        copy.wait()
    landed = x2r[...].reshape(256, LANES).T
    first = pick(landed, perm[0])
    wind = pick(landed[0:PAD], perm[1])
    target = [first[0:PAD], first[PAD:128]]
    speeds = jnp.where(level == PAD - 1, 1.0, 0.125 * jnp.tanh(wind))
    columns = jnp.concatenate([speeds] + [0.5 * (target[f] - moved_mean[f]) for f in range(2)], axis=0)
    hi, lo = split(columns, 2)
    coef[0] = hi
    coef[1] = lo
    col256 = iota((LANES, 256), 1)
    twice = hot(iota((LANES, 256), 0) == (col256 // 8) * GROUP + col256 % GROUP)
    coef_rows[...] = pick(columns, twice).T.reshape(GROUPS, 8, 3 * PAD)

    def send_coef(i, carry):
        g, h = slots_for(peer(gy, i, 1))
        first_half = jnp.where(g >= 0, coef_rows[jnp.maximum(g, 0)], 0.0)
        second_half = jnp.where(h >= 0, coef_rows[jnp.maximum(h, 0)], 0.0)
        c6s[i] = jnp.where(iota((8, 3 * PAD), 0) < GROUP, first_half, second_half)
        coef_copy(i).start()
        return carry
    lax.fori_loop(0, RAW, send_coef, 0)
    lax.fori_loop(WAVES[1], WAVES[2], send_raw, 0)

    def spread_out(i, carry):
        lanes = pl.ds(pl.multiple_of(i * 512, 512), 512)
        e = spread_of[:, lanes]
        spread[:, lanes] = dot(coef[0], e, NN) + dot(coef[1], e, NN)
        return carry
    lax.fori_loop(0, 8, spread_out, 0)

    x = iota((PAD, LANES), 1) % CRM_X

    def advance(s, speed, shift):
        west = jnp.where(x == 0, pltpu.roll(s, LANES - 31, 1), pltpu.roll(s, 1, 1))
        east = jnp.where(x == CRM_X - 1, pltpu.roll(s, 31, 1), pltpu.roll(s, LANES - 1, 1))
        return (0.6 * s + 0.1 * ((east + west) + (below(s) + above(s))) - speed * (east - west)) + shift

    def physics(s0, s1, speed, shift0, shift1):
        energy = advance(padded(s0), speed, shift0)
        water = advance(padded(s1), speed, shift1)
        base = 0.5 * energy + (1.25 * water - 0.625)
        half = base - 0.625 * jnp.tanh(0.5 * energy)
        half = base - 0.625 * jnp.tanh(half)
        half = base - 0.625 * jnp.tanh(half)
        return energy, 0.8 * water + (0.1 + 0.1 * jnp.tanh(half)), half

    def one_group(g, carry):
        lanes = pl.ds(pl.multiple_of(g * LANES, LANES), LANES)
        energy, final, half = physics(
            groups[g, 0], groups[g, 1],
            spread[0:PAD, lanes], spread[PAD:2 * PAD, lanes], spread[2 * PAD:3 * PAD, lanes])
        warm[0, :, lanes] = half + half
        warm[1, :, lanes] = final
        fin[g, 0] = energy[0:LEV]
        fin[g, 1] = final[0:LEV]
        return carry
    lax.fori_loop(0, GROUPS, one_group, 0)

    ends = column_means(lambda f, lanes: warm[f, :, lanes], mean_sc)
    tendency = ends - first
    back = hot((row // 8 == col % 32) & (row % 8 == col // 32))
    r1s[...] = pick_rows(back, tendency, NT).reshape(32, 8, LANES)[:, 0:NX]
    stage3 = []
    for i, ty in enumerate(peers_y):
        copy = pltpu.make_async_remote_copy(
            src_ref=r1s.at[ty], dst_ref=r1r.at[gy],
            send_sem=s3.at[i], recv_sem=v3.at[i], device_id={"gy": ty}, device_id_type=MESH,
        )
        copy.start()
        stage3.append(copy)
    r1r[gy] = r1s[gy]

    def send_final(i, carry):
        gather(i, peer(gy, i, 1), fin)
        state_copy(i).start()
        return carry
    lax.fori_loop(RAW, NY - 1, send_final, 0)
    gather(31, gy, fin)
    own = pltpu.make_async_copy(send.at[31], out_ref.at[:, :, own_lanes], own_sem)
    own.start()

    def wait_coef(i, carry):
        coef_copy(i).wait()
        return carry
    lax.fori_loop(0, RAW, wait_coef, 0)
    came = split(c6r[...].reshape(RAW * 8, 3 * PAD).T, 2)

    def finish(i, carry):
        state_copy(i).wait()
        e = hot(iota((RAW * 8, 256), 0) == i * 8 + iota((RAW * 8, 256), 1) // CRM_X)
        both = dot(came[0], e, NN) + dot(came[1], e, NN)
        start = peer(gy, i, -1) * 256
        for r in range(2):
            c = both[:, r * LANES:(r + 1) * LANES]
            lanes = pl.ds(pl.multiple_of(start + r * LANES, LANES), LANES)
            energy, final, _ = physics(
                out_ref[:, 0, lanes], out_ref[:, 1, lanes], c[0:PAD], c[PAD:2 * PAD], c[2 * PAD:3 * PAD])
            out_ref[:, 0, lanes] = energy[0:LEV]
            out_ref[:, 1, lanes] = (c[PAD - 1:PAD] * final)[0:LEV]
        return carry
    lax.fori_loop(0, RAW, finish, 0)

    for copy in stage3:
        copy.wait()
    rows = iota((LANES, 256), 0)
    cols = iota((LANES, 256), 1)
    r2s[...] = pick_rows(
        hot((rows % 32 == cols // 8) & (rows // 32 == cols % 8)),
        jnp.concatenate([r1r[...], jnp.zeros((NY, 8 - NX, LANES), F32)], axis=1).reshape(256, LANES))
    stage4 = []
    for i, tx in enumerate(peers_x):
        copy = pltpu.make_async_remote_copy(
            src_ref=r2s.at[pl.ds(pl.multiple_of(tx * 32, 32), 32), :], dst_ref=r2r.at[own_rows, :],
            send_sem=s4.at[i], recv_sem=v4.at[i], device_id={"gx": tx}, device_id_type=MESH,
        )
        copy.start()
        stage4.append(copy)
    r2r[own_rows, :] = r2s[own_rows, :]
    for copy in stage4:
        copy.wait()
    placed = pick(r2r[...].T, chosen, NT)
    tend_ref[:, 0, :] = placed[0:LEV]
    tend_ref[:, 1, :] = placed[PAD:PAD + LEV]

    own.wait()

    def wait_final(i, carry):
        state_copy(i).wait()
        return carry
    lax.fori_loop(RAW, NY - 1, wait_final, 0)


def on_device(gcm_state, crm_state, send_source, group_owner):
    vm = pltpu.VMEM
    dma = pltpu.SemaphoreType.DMA
    hbm = pl.BlockSpec(memory_space=pltpu.HBM)
    vmem = pl.BlockSpec(memory_space=pltpu.VMEM)
    crm_next, tendency = pl.pallas_call(
        step_kernel,
        out_shape=(jax.ShapeDtypeStruct((LEV, 2, 8192), F32), jax.ShapeDtypeStruct((LEV, 2, LANES), F32)),
        in_specs=[hbm] * 4,
        out_specs=(vmem, vmem),
        scratch_shapes=[
            vm((LEV, 2, 4096), F32), vm((GROUPS, 2, LEV, LANES), F32), vm((3, LEV, LANES), F32), vm((1, LANES), jnp.int32), vm((4, PAD, LANES), F32),
            vm((2, 128, LANES), F32), vm((2, 128, LANES), F32),
            vm((32, 8, LANES), F32), vm((32, 8, LANES), F32),
            vm((32, NX, LANES), F32), vm((32, NX, LANES), F32),
            vm((128, LANES), F32), vm((128, LANES), F32),
            vm((3 * PAD, 4096), F32), vm((LANES, 4096), BF16),
            vm((GROUPS, 2, LEV, LANES), F32), vm((2, PAD, 4096), F32),
            vm((32, LEV, 2, 256), F32), vm((2 * PAD, LANES), F32), vm((2, 3 * PAD, LANES), BF16),
            vm((RAW, 8, 3 * PAD), F32), vm((RAW, 8, 3 * PAD), F32), vm((GROUPS, 8, 3 * PAD), F32),
            pltpu.SMEM((GROUPS,), jnp.int32), dma, dma, dma, dma, dma, dma((3,)), dma((3,)), dma((31,)), dma((31,)), dma((31,)), dma((31,)),
            dma((3,)), dma((3,)), dma((31,)), dma((31,)), dma((RAW,)), dma((RAW,)),
        ],
        compiler_params=pltpu.CompilerParams(collective_id=0, has_side_effects=True, vmem_limit_bytes=48 << 20),
    )(*[pltpu.with_memory_space_constraint(a, pltpu.HBM) for a in (
        group_owner, send_source.reshape(1, LANES), gcm_state, crm_state.transpose(1, 0, 2))])
    return tendency.transpose(1, 0, 2), crm_next.transpose(1, 0, 2)


def solution(mesh):
    spec = P(None, None, ("gx", "gy"))
    flat = P(("gx", "gy"))
    return jax.shard_map(
        on_device, mesh=mesh, in_specs=(spec, spec, flat, flat), out_specs=(spec, spec), check_vma=False)
```

```python
import functools

import jax
import jax.numpy as jnp
from jax import lax
from jax.experimental import pallas as pl
from jax.experimental.pallas import tpu as pltpu
from jax.sharding import PartitionSpec as P

CRM_X = 32
LEV = 58
PAD = 64
LANES = 128
NX = 4
NY = 32
GROUPS = 32
GROUP = 4
F32 = jnp.float32
BF16 = jnp.bfloat16
MESH = pl.DeviceIdType.MESH

NN = (((1,), (0,)), ((), ()))
NT = (((1,), (1,)), ((), ()))

RAW = 16
WAVES = (2, 12, RAW, RAW)
STRIDE = 13


def peer(gy, i, sign):
    offset = (STRIDE * (i + 1)) % NY
    other = (gy + offset) % 2
    second = gy % 2 if sign > 0 else other
    dz, dy = offset // 8, (offset // 2) % 4
    step_z = dz * (1 - 2 * second)
    step_y = dy
    z = (gy // 8 + 4 + sign * step_z) % 4
    y = ((gy // 2) % 4 + 4 + sign * step_y) % 4
    return (z * 4 + y) * 2 + other


def split(x, pieces):
    out = []
    for _ in range(pieces - 1):
        hi = x.astype(BF16)
        out.append(hi)
        x = x - hi.astype(F32)
    out.append(x.astype(BF16))
    return out


def dot(a, b, dims):
    return lax.dot_general(a, b, dims, preferred_element_type=F32)


def pick(x, onehot, dims=NN):
    parts = [dot(p, onehot, dims) for p in split(x, 3)]
    return parts[0] + (parts[1] + parts[2])


def pick_rows(onehot, x, dims=NN):
    parts = [dot(onehot, p, dims) for p in split(x, 3)]
    return parts[0] + (parts[1] + parts[2])


def iota(shape, dim):
    return lax.broadcasted_iota(jnp.int32, shape, dim)


def hot(cond):
    return jnp.where(cond, 1.0, 0.0).astype(BF16)


def padded(s):
    if s.shape[0] == PAD:
        return s
    return jnp.concatenate([s, jnp.zeros((PAD - LEV, s.shape[1]), F32)], axis=0)


def step_kernel(
    owner_hbm, source_hbm, gcm_hbm, crm_hbm,
    out_ref, tend_ref,
    crm, gcm, source_of, gpad, x1s, x1r, x2s, x2r, r1s, r1r, r2s, r2r, spread, spread_of, fin, warm, send, mean_sc, coef,
    c6s, c6r, coef_rows, raw,
    owner, crm_sem, owner_sem, gcm_sem, source_sem, own_sem, s1, v1, s2, v2, s3, v3, s4, v4, s5, v5, s6, v6,
):
    gx = lax.axis_index("gx")
    gy = lax.axis_index("gy")
    peers_x = [(gx + d) % NX for d in (1, 2, 3)]

    barrier = pltpu.get_barrier_semaphore()
    for tx in peers_x:
        pl.semaphore_signal(barrier, inc=1, device_id={"gx": tx}, device_id_type=MESH)
    for i in range(NY - 1):
        pl.semaphore_signal(barrier, inc=1, device_id={"gy": peer(gy, i, 1)}, device_id_type=MESH)

    gcm_load = pltpu.make_async_copy(gcm_hbm, gcm, gcm_sem)
    source_load = pltpu.make_async_copy(source_hbm, source_of, source_sem)
    owner_load = pltpu.make_async_copy(owner_hbm, owner, owner_sem)
    gcm_load.start()
    source_load.start()
    owner_load.start()

    def group_load(g):
        lanes = pl.ds(pl.multiple_of(g * LANES, LANES), LANES)
        return pltpu.make_async_copy(crm_hbm.at[:, :, lanes], crm.at[g, pl.ds(1, LEV)], crm_sem.at[g])

    def start_load(g, carry):
        group_load(g).start()
        return carry
    lax.fori_loop(0, GROUPS, start_load, 0)

    gpad[...] = jnp.zeros((4, PAD, LANES), F32)
    gcm_load.wait()
    source_load.wait()
    gpad[0:3, 0:LEV, :] = gcm[...]
    chosen = hot(iota((LANES, LANES), 0) == source_of[...])
    packed = pick(gpad[...].reshape(4 * PAD, LANES), chosen)
    x1s[0] = packed[0:128].T
    x1s[1] = packed[128:256].T
    own_rows = pl.ds(pl.multiple_of(gx * 32, 32), 32)

    pl.semaphore_wait(barrier, 3 + 31)
    stage1 = []
    for i, tx in enumerate(peers_x):
        copy = pltpu.make_async_remote_copy(
            src_ref=x1s.at[:, pl.ds(pl.multiple_of(tx * 32, 32), 32), :],
            dst_ref=x1r.at[:, own_rows, :],
            send_sem=s1.at[i], recv_sem=v1.at[i], device_id={"gx": tx}, device_id_type=MESH,
        )
        copy.start()
        stage1.append(copy)

    own_lanes = pl.ds(pl.multiple_of(gy * 256, 256), 256)

    def state_copy(i):
        return pltpu.make_async_remote_copy(
            src_ref=send.at[i], dst_ref=out_ref.at[:, :, own_lanes],
            send_sem=s5.at[i], recv_sem=v5.at[i], device_id={"gy": peer(gy, i, 1)}, device_id_type=MESH,
        )

    def raw_copy(i):
        return pltpu.make_async_remote_copy(
            src_ref=send.at[i], dst_ref=raw.at[i, pl.ds(1, LEV)],
            send_sem=s5.at[i], recv_sem=v5.at[i], device_id={"gy": peer(gy, i, 1)}, device_id_type=MESH,
        )

    def column_copy(i):
        return pltpu.make_async_remote_copy(
            src_ref=x2s.at[peer(gy, i, 1)], dst_ref=x2r.at[gy],
            send_sem=s2.at[i], recv_sem=v2.at[i], device_id={"gy": peer(gy, i, 1)}, device_id_type=MESH,
        )

    def tendency_copy(i):
        return pltpu.make_async_remote_copy(
            src_ref=r1s.at[peer(gy, i, 1)], dst_ref=r1r.at[gy],
            send_sem=s3.at[i], recv_sem=v3.at[i], device_id={"gy": peer(gy, i, 1)}, device_id_type=MESH,
        )

    def coef_copy(i):
        return pltpu.make_async_remote_copy(
            src_ref=c6s.at[i], dst_ref=c6r.at[i],
            send_sem=s6.at[i], recv_sem=v6.at[i], device_id={"gy": peer(gy, i, 1)}, device_id_type=MESH,
        )

    def slots_for(d):
        low, high = jnp.int32(GROUPS), jnp.int32(-1)
        for g in range(GROUPS):
            same = owner[g] == d
            low = jnp.minimum(low, jnp.where(same, g, GROUPS))
            high = jnp.where(same, g, high)
        return jnp.where(high < 0, -1, low), jnp.where(high > low, high, -1)

    def send_raw(i, carry):
        for r, g in enumerate(slots_for(peer(gy, i, 1))):
            send[i, :, :, r * LANES:(r + 1) * LANES] = jnp.where(g >= 0, crm[jnp.maximum(g, 0)][1:1 + LEV], 0.0)
        raw_copy(i).start()
        return carry

    def wait_load(g, carry):
        group_load(g).wait()
        return carry
    owner_load.wait()
    lax.fori_loop(0, GROUPS, wait_load, 0)
    lax.fori_loop(0, WAVES[0], send_raw, 0)

    def fill(g, carry):
        cols = g * GROUP + iota((LANES, LANES), 1) // CRM_X
        spread_of[:, pl.ds(pl.multiple_of(g * LANES, LANES), LANES)] = hot(iota((LANES, LANES), 0) == cols)
        return carry
    lax.fori_loop(0, GROUPS, fill, 0)
    row = iota((256, LANES), 0)
    col = iota((256, LANES), 1)
    here = (row // 8 == col % 32)
    perm = [hot(here & (row % 8 == (col // 32) * 2 + h)) for h in range(2)]

    x1r[:, own_rows, :] = x1s[:, own_rows, :]
    for copy in stage1:
        copy.wait()
    x2s[...] = (pick_rows(perm[0], x1r[0]) + pick_rows(perm[1], x1r[1])).reshape(32, 8, LANES)
    for i in range(NY - 1):
        column_copy(i).start()
    x2r[gy] = x2s[gy]
    lax.fori_loop(WAVES[0], WAVES[1], send_raw, 0)

    mean_sc[...] = jnp.zeros((2 * PAD, LANES), F32)

    def repeat_ends(ref, i):
        ref[i, 0:1] = ref[i, 1:2]
        ref[i, LEV + 1:LEV + 2] = ref[i, LEV:LEV + 1]

    def add_mean(i, carry):
        total = mean_sc[...]
        for h in range(2):
            g = i * 2 + h
            repeat_ends(crm, g)
            fields = [padded(crm[g, pl.ds(1, LEV), f, :]) for f in range(2)]
            hi, lo = split(jnp.concatenate(fields, axis=0), 2)
            e = spread_of[:, pl.ds(pl.multiple_of(g * LANES, LANES), LANES)]
            total = total + (dot(hi, e, NT) + dot(lo, e, NT))
        mean_sc[...] = total
        return carry
    lax.fori_loop(0, GROUPS // 2, add_mean, 0)
    means = mean_sc[...] * (1.0 / CRM_X)
    level = iota((PAD, LANES), 0)

    def below(s):
        return jnp.where(level == 0, s, pltpu.roll(s, 1, 0))

    def above(s):
        return jnp.where(level == LEV - 1, s, pltpu.roll(s, PAD - 1, 0))

    moved_mean = []
    for f in range(2):
        m = means[f * PAD:(f + 1) * PAD]
        moved_mean.append(0.8 * m + 0.1 * (below(m) + above(m)))

    for i in range(NY - 1):
        column_copy(i).wait()
    landed = x2r[...].reshape(256, LANES).T
    first = pick(landed, perm[0])
    wind = pick(landed[0:PAD], perm[1])
    target = [first[0:PAD], first[PAD:128]]
    speeds = jnp.where(level == PAD - 1, 1.0, 0.125 * jnp.tanh(wind))
    columns = jnp.concatenate([speeds] + [0.5 * (target[f] - moved_mean[f]) for f in range(2)], axis=0)
    hi, lo = split(columns, 2)
    coef[0] = hi
    coef[1] = lo
    col256 = iota((LANES, 256), 1)
    twice = hot(iota((LANES, 256), 0) == (col256 // 8) * GROUP + col256 % GROUP)
    coef_rows[...] = pick(columns, twice).T.reshape(GROUPS, 8, 3 * PAD)

    def send_coef(i, carry):
        g, h = slots_for(peer(gy, i, 1))
        first_half = jnp.where(g >= 0, coef_rows[jnp.maximum(g, 0)], 0.0)
        second_half = jnp.where(h >= 0, coef_rows[jnp.maximum(h, 0)], 0.0)
        c6s[i] = jnp.where(iota((8, 3 * PAD), 0) < GROUP, first_half, second_half)
        coef_copy(i).start()
        return carry
    lax.fori_loop(0, RAW, send_coef, 0)
    lax.fori_loop(WAVES[1], WAVES[2], send_raw, 0)
    x = iota((PAD, LANES), 1) % CRM_X

    def advance(read, speed, shift):
        s = padded(read(1))
        west = jnp.where(x == 0, pltpu.roll(s, LANES - 31, 1), pltpu.roll(s, 1, 1))
        east = jnp.where(x == CRM_X - 1, pltpu.roll(s, 31, 1), pltpu.roll(s, LANES - 1, 1))
        return (0.6 * s + 0.1 * ((east + west) + (padded(read(0)) + padded(read(2)))) - speed * (east - west)) + shift

    def physics(ref, i, lanes, speed, shift0, shift1):
        energy = advance(lambda k: ref[i, pl.ds(k, LEV), 0, lanes], speed, shift0)
        water = advance(lambda k: ref[i, pl.ds(k, LEV), 1, lanes], speed, shift1)
        base = 0.5 * energy + (1.25 * water - 0.625)
        half = base - 0.625 * jnp.tanh(0.5 * energy)
        half = base - 0.625 * jnp.tanh(half)
        half = base - 0.625 * jnp.tanh(half)
        return energy, 0.8 * water + (0.1 + 0.1 * jnp.tanh(half)), half

    def spread_out(i, slot):
        e = spread_of[:, pl.ds(pl.multiple_of(i * 256, 256), 256)]
        spread[slot] = dot(coef[0], e, NN) + dot(coef[1], e, NN)
    spread_out(0, 0)

    def two_groups(i, carry):
        slot = i % 2
        spread_out((i + 1) % (GROUPS // 2), (i + 1) % 2)
        for h in range(2):
            g = i * 2 + h
            c = slice(h * LANES, (h + 1) * LANES)
            energy, final, half = physics(
                crm, g, slice(None),
                spread[slot, 0:PAD, c], spread[slot, PAD:2 * PAD, c], spread[slot, 2 * PAD:3 * PAD, c])
            lanes = pl.ds(pl.multiple_of(g * LANES, LANES), LANES)
            warm[0, :, lanes] = half + half
            warm[1, :, lanes] = final
            fin[g, 0] = energy[0:LEV]
            fin[g, 1] = final[0:LEV]
        return carry
    lax.fori_loop(0, GROUPS // 2, two_groups, 0)

    def gather(i, d):
        for r, g in enumerate(slots_for(d)):
            block = fin[jnp.maximum(g, 0)]
            block = jnp.where(g >= 0, block, 0.0)
            for f in range(2):
                send[i, :, f, r * LANES:(r + 1) * LANES] = block[f]

    def send_final(i, carry):
        gather(i, peer(gy, i, 1))
        state_copy(i).start()
        return carry
    lax.fori_loop(WAVES[2], WAVES[3], send_final, 0)

    mean_sc[...] = jnp.zeros((2 * PAD, LANES), F32)

    def add_end(i, carry):
        lanes = pl.ds(pl.multiple_of(i * 512, 512), 512)
        hi, lo = split(jnp.concatenate([warm[0, :, lanes], warm[1, :, lanes]], axis=0), 2)
        e = spread_of[:, lanes]
        mean_sc[...] += dot(hi, e, NT) + dot(lo, e, NT)
        return carry
    lax.fori_loop(0, 8, add_end, 0)
    tendency = mean_sc[...] * (1.0 / CRM_X) - first
    back = hot((row // 8 == col % 32) & (row % 8 == col // 32))
    r1s[...] = pick_rows(back, tendency, NT).reshape(32, 8, LANES)[:, 0:NX]
    for i in range(NY - 1):
        tendency_copy(i).start()
    r1r[gy] = r1s[gy]

    lax.fori_loop(WAVES[3], NY - 1, send_final, 0)
    gather(31, gy)
    own = pltpu.make_async_copy(send.at[31], out_ref.at[:, :, own_lanes], own_sem)
    own.start()

    def take_coef(i, carry):
        coef_copy(i).wait()
        return carry
    lax.fori_loop(0, RAW, take_coef, 0)
    came = split(c6r[...].reshape(RAW * 8, 3 * PAD).T, 2)

    def finish(i, carry):
        raw_copy(i).wait()
        repeat_ends(raw, i)
        e = hot(iota((RAW * 8, 256), 0) == i * 8 + iota((RAW * 8, 256), 1) // CRM_X)
        both = dot(came[0], e, NN) + dot(came[1], e, NN)
        start = peer(gy, i, -1) * 256
        for r in range(2):
            c = both[:, r * LANES:(r + 1) * LANES]
            lanes = pl.ds(pl.multiple_of(start + r * LANES, LANES), LANES)
            energy, final, _ = physics(
                raw, i, slice(r * LANES, (r + 1) * LANES), c[0:PAD], c[PAD:2 * PAD], c[2 * PAD:3 * PAD])
            out_ref[:, 0, lanes] = energy[0:LEV]
            out_ref[:, 1, lanes] = (c[PAD - 1:PAD] * final)[0:LEV]
        return carry
    lax.fori_loop(0, RAW, finish, 0)

    for i in range(NY - 1):
        tendency_copy(i).wait()
    rows = iota((LANES, 256), 0)
    cols = iota((LANES, 256), 1)
    r2s[...] = pick_rows(
        hot((rows % 32 == cols // 8) & (rows // 32 == cols % 8)),
        jnp.concatenate([r1r[...], jnp.zeros((NY, 8 - NX, LANES), F32)], axis=1).reshape(256, LANES))
    stage4 = []
    for i, tx in enumerate(peers_x):
        copy = pltpu.make_async_remote_copy(
            src_ref=r2s.at[pl.ds(pl.multiple_of(tx * 32, 32), 32), :], dst_ref=r2r.at[own_rows, :],
            send_sem=s4.at[i], recv_sem=v4.at[i], device_id={"gx": tx}, device_id_type=MESH,
        )
        copy.start()
        stage4.append(copy)
    r2r[own_rows, :] = r2s[own_rows, :]

    for copy in stage4:
        copy.wait()
    placed = pick(r2r[...].T, chosen, NT)
    tend_ref[:, 0, :] = placed[0:LEV]
    tend_ref[:, 1, :] = placed[PAD:PAD + LEV]

    own.wait()

    def wait_final(i, carry):
        state_copy(i).wait()
        return carry
    lax.fori_loop(RAW, NY - 1, wait_final, 0)


def on_device(gcm_state, crm_state, send_source, group_owner):
    vm = pltpu.VMEM
    dma = pltpu.SemaphoreType.DMA
    hbm = pl.BlockSpec(memory_space=pltpu.HBM)
    vmem = pl.BlockSpec(memory_space=pltpu.VMEM)
    crm_next, tendency = pl.pallas_call(
        step_kernel,
        out_shape=(jax.ShapeDtypeStruct((LEV, 2, 8192), F32), jax.ShapeDtypeStruct((LEV, 2, LANES), F32)),
        in_specs=[hbm] * 4,
        out_specs=(vmem, vmem),
        scratch_shapes=[
            vm((GROUPS, LEV + 2, 2, LANES), F32), vm((3, LEV, LANES), F32), vm((1, LANES), jnp.int32), vm((4, PAD, LANES), F32),
            vm((2, 128, LANES), F32), vm((2, 128, LANES), F32),
            vm((32, 8, LANES), F32), vm((32, 8, LANES), F32),
            vm((32, NX, LANES), F32), vm((32, NX, LANES), F32),
            vm((128, LANES), F32), vm((128, LANES), F32),
            vm((2, 3 * PAD, 256), F32), vm((LANES, 4096), BF16),
            vm((GROUPS, 2, LEV, LANES), F32), vm((2, PAD, 4096), F32),
            vm((32, LEV, 2, 256), F32), vm((2 * PAD, LANES), F32), vm((2, 3 * PAD, LANES), BF16),
            vm((RAW, 8, 3 * PAD), F32), vm((RAW, 8, 3 * PAD), F32), vm((GROUPS, 8, 3 * PAD), F32), vm((RAW, LEV + 2, 2, 256), F32),
            pltpu.SMEM((GROUPS,), jnp.int32), dma((GROUPS,)), dma, dma, dma, dma, dma((3,)), dma((3,)), dma((31,)), dma((31,)), dma((31,)), dma((31,)),
            dma((3,)), dma((3,)), dma((31,)), dma((31,)), dma((RAW,)), dma((RAW,)),
        ],
        compiler_params=pltpu.CompilerParams(collective_id=0, has_side_effects=True, vmem_limit_bytes=48 << 20),
    )(*[pltpu.with_memory_space_constraint(a, pltpu.HBM) for a in (
        group_owner, send_source.reshape(1, LANES), gcm_state, crm_state.transpose(1, 0, 2))])
    return tendency.transpose(1, 0, 2), crm_next.transpose(1, 0, 2)


def solution(mesh):
    spec = P(None, None, ("gx", "gy"))
    flat = P(("gx", "gy"))
    return jax.shard_map(
        on_device, mesh=mesh, in_specs=(spec, spec, flat, flat), out_specs=(spec, spec), check_vma=False)
```

```python
import functools

import jax
import jax.numpy as jnp
from jax import lax
from jax.experimental import pallas as pl
from jax.experimental.pallas import tpu as pltpu
from jax.sharding import PartitionSpec as P

CRM_X = 32
LEV = 58
PAD = 64
LANES = 128
NX = 4
NY = 32
GROUPS = 32
GROUP = 4
F32 = jnp.float32
BF16 = jnp.bfloat16
MESH = pl.DeviceIdType.MESH

NN = (((1,), (0,)), ((), ()))
NT = (((1,), (1,)), ((), ()))

RAW = 16
WAVES = (2, 12, RAW, RAW)
STRIDE = 13


def peer(gy, i, sign):
    offset = (STRIDE * (i + 1)) % NY
    other = (gy + offset) % 2
    second = gy % 2 if sign > 0 else other
    dz, dy = offset // 8, (offset // 2) % 4
    step_z = dz * (1 - 2 * second)
    step_y = dy
    z = (gy // 8 + 4 + sign * step_z) % 4
    y = ((gy // 2) % 4 + 4 + sign * step_y) % 4
    return (z * 4 + y) * 2 + other


def split(x, pieces):
    out = []
    for _ in range(pieces - 1):
        hi = x.astype(BF16)
        out.append(hi)
        x = x - hi.astype(F32)
    out.append(x.astype(BF16))
    return out


def dot(a, b, dims):
    return lax.dot_general(a, b, dims, preferred_element_type=F32)


def pick(x, onehot, dims=NN):
    parts = [dot(p, onehot, dims) for p in split(x, 3)]
    return parts[0] + (parts[1] + parts[2])


def pick_rows(onehot, x, dims=NN):
    parts = [dot(onehot, p, dims) for p in split(x, 3)]
    return parts[0] + (parts[1] + parts[2])


def iota(shape, dim):
    return lax.broadcasted_iota(jnp.int32, shape, dim)


def hot(cond):
    return jnp.where(cond, 1.0, 0.0).astype(BF16)


def padded(s):
    if s.shape[0] == PAD:
        return s
    return jnp.concatenate([s, jnp.zeros((PAD - LEV, s.shape[1]), F32)], axis=0)


def step_kernel(
    owner_hbm, source_hbm, gcm_hbm, crm_hbm,
    out_ref, tend_ref,
    crm, gcm, source_of, gpad, x1s, x1r, x2s, x2r, r1s, r1r, r2s, r2r, spread, spread_of, fin, warm, send, mean_sc, coef,
    c6s, c6r, coef_rows, raw,
    owner, crm_sem, owner_sem, gcm_sem, source_sem, own_sem, s1, v1, s2, v2, s3, v3, s4, v4, s5, v5, s6, v6,
):
    gx = lax.axis_index("gx")
    gy = lax.axis_index("gy")
    peers_x = [(gx + d) % NX for d in (1, 2, 3)]

    barrier = pltpu.get_barrier_semaphore()
    for tx in peers_x:
        pl.semaphore_signal(barrier, inc=1, device_id={"gx": tx}, device_id_type=MESH)
    for i in range(NY - 1):
        pl.semaphore_signal(barrier, inc=1, device_id={"gy": peer(gy, i, 1)}, device_id_type=MESH)

    gcm_load = pltpu.make_async_copy(gcm_hbm, gcm, gcm_sem)
    source_load = pltpu.make_async_copy(source_hbm, source_of, source_sem)
    owner_load = pltpu.make_async_copy(owner_hbm, owner, owner_sem)
    gcm_load.start()
    source_load.start()
    owner_load.start()

    def group_load(g):
        lanes = pl.ds(pl.multiple_of(g * LANES, LANES), LANES)
        return pltpu.make_async_copy(crm_hbm.at[:, :, lanes], crm.at[g, pl.ds(1, LEV)], crm_sem.at[g])

    def start_load(g, carry):
        group_load(g).start()
        return carry
    lax.fori_loop(0, GROUPS, start_load, 0)

    gpad[...] = jnp.zeros((4, PAD, LANES), F32)
    gcm_load.wait()
    source_load.wait()
    gpad[0:3, 0:LEV, :] = gcm[...]
    chosen = hot(iota((LANES, LANES), 0) == source_of[...])
    packed = pick(gpad[...].reshape(4 * PAD, LANES), chosen)
    x1s[0] = packed[0:128].T
    x1s[1] = packed[128:256].T
    own_rows = pl.ds(pl.multiple_of(gx * 32, 32), 32)

    pl.semaphore_wait(barrier, 3 + 31)
    stage1 = []
    for i, tx in enumerate(peers_x):
        copy = pltpu.make_async_remote_copy(
            src_ref=x1s.at[:, pl.ds(pl.multiple_of(tx * 32, 32), 32), :],
            dst_ref=x1r.at[:, own_rows, :],
            send_sem=s1.at[i], recv_sem=v1.at[i], device_id={"gx": tx}, device_id_type=MESH,
        )
        copy.start()
        stage1.append(copy)

    own_lanes = pl.ds(pl.multiple_of(gy * 256, 256), 256)

    def state_copy(i):
        return pltpu.make_async_remote_copy(
            src_ref=send.at[i], dst_ref=out_ref.at[:, :, own_lanes],
            send_sem=s5.at[i], recv_sem=v5.at[i], device_id={"gy": peer(gy, i, 1)}, device_id_type=MESH,
        )

    def raw_copy(i):
        return pltpu.make_async_remote_copy(
            src_ref=send.at[i], dst_ref=raw.at[i, pl.ds(1, LEV)],
            send_sem=s5.at[i], recv_sem=v5.at[i], device_id={"gy": peer(gy, i, 1)}, device_id_type=MESH,
        )

    def column_copy(i):
        return pltpu.make_async_remote_copy(
            src_ref=x2s.at[peer(gy, i, 1)], dst_ref=x2r.at[gy],
            send_sem=s2.at[i], recv_sem=v2.at[i], device_id={"gy": peer(gy, i, 1)}, device_id_type=MESH,
        )

    def tendency_copy(i):
        return pltpu.make_async_remote_copy(
            src_ref=r1s.at[peer(gy, i, 1)], dst_ref=r1r.at[gy],
            send_sem=s3.at[i], recv_sem=v3.at[i], device_id={"gy": peer(gy, i, 1)}, device_id_type=MESH,
        )

    def coef_copy(i):
        return pltpu.make_async_remote_copy(
            src_ref=c6s.at[i], dst_ref=c6r.at[i],
            send_sem=s6.at[i], recv_sem=v6.at[i], device_id={"gy": peer(gy, i, 1)}, device_id_type=MESH,
        )

    def slots_for(d):
        low, high = jnp.int32(GROUPS), jnp.int32(-1)
        for g in range(GROUPS):
            same = owner[g] == d
            low = jnp.minimum(low, jnp.where(same, g, GROUPS))
            high = jnp.where(same, g, high)
        return jnp.where(high < 0, -1, low), jnp.where(high > low, high, -1)

    def send_raw(i, carry):
        for r, g in enumerate(slots_for(peer(gy, i, 1))):
            send[i, :, :, r * LANES:(r + 1) * LANES] = jnp.where(g >= 0, crm[jnp.maximum(g, 0)][1:1 + LEV], 0.0)
        raw_copy(i).start()
        return carry

    def wait_load(g, carry):
        group_load(g).wait()
        return carry
    owner_load.wait()
    lax.fori_loop(0, GROUPS, wait_load, 0)
    lax.fori_loop(0, WAVES[0], send_raw, 0)

    def fill(g, carry):
        cols = g * GROUP + iota((LANES, LANES), 1) // CRM_X
        spread_of[:, pl.ds(pl.multiple_of(g * LANES, LANES), LANES)] = hot(iota((LANES, LANES), 0) == cols)
        return carry
    lax.fori_loop(0, GROUPS, fill, 0)
    row = iota((256, LANES), 0)
    col = iota((256, LANES), 1)
    here = (row // 8 == col % 32)
    perm = [hot(here & (row % 8 == (col // 32) * 2 + h)) for h in range(2)]

    x1r[:, own_rows, :] = x1s[:, own_rows, :]
    for copy in stage1:
        copy.wait()
    x2s[...] = (pick_rows(perm[0], x1r[0]) + pick_rows(perm[1], x1r[1])).reshape(32, 8, LANES)
    for i in range(NY - 1):
        column_copy(i).start()
    x2r[gy] = x2s[gy]
    lax.fori_loop(WAVES[0], WAVES[1], send_raw, 0)

    mean_sc[...] = jnp.zeros((2 * PAD, LANES), F32)

    def repeat_ends(ref, i):
        ref[i, 0:1] = ref[i, 1:2]
        ref[i, LEV + 1:LEV + 2] = ref[i, LEV:LEV + 1]

    def add_mean(i, carry):
        total = mean_sc[...]
        for h in range(2):
            g = i * 2 + h
            repeat_ends(crm, g)
            fields = [padded(crm[g, pl.ds(1, LEV), f, :]) for f in range(2)]
            hi, lo = split(jnp.concatenate(fields, axis=0), 2)
            e = spread_of[:, pl.ds(pl.multiple_of(g * LANES, LANES), LANES)]
            total = total + (dot(hi, e, NT) + dot(lo, e, NT))
        mean_sc[...] = total
        return carry
    lax.fori_loop(0, GROUPS // 2, add_mean, 0)
    means = mean_sc[...] * (1.0 / CRM_X)
    level = iota((PAD, LANES), 0)

    def below(s):
        return jnp.where(level == 0, s, pltpu.roll(s, 1, 0))

    def above(s):
        return jnp.where(level == LEV - 1, s, pltpu.roll(s, PAD - 1, 0))

    moved_mean = []
    for f in range(2):
        m = means[f * PAD:(f + 1) * PAD]
        moved_mean.append(0.8 * m + 0.1 * (below(m) + above(m)))

    for i in range(NY - 1):
        column_copy(i).wait()
    landed = x2r[...].reshape(256, LANES).T
    first = pick(landed, perm[0])
    wind = pick(landed[0:PAD], perm[1])
    target = [first[0:PAD], first[PAD:128]]
    speeds = jnp.where(level == PAD - 1, 1.0, 0.125 * jnp.tanh(wind))
    columns = jnp.concatenate([speeds] + [0.5 * (target[f] - moved_mean[f]) for f in range(2)], axis=0)
    hi, lo = split(columns, 2)
    coef[0] = hi
    coef[1] = lo
    col256 = iota((LANES, 256), 1)
    twice = hot(iota((LANES, 256), 0) == (col256 // 8) * GROUP + col256 % GROUP)
    coef_rows[...] = pick(columns, twice).T.reshape(GROUPS, 8, 3 * PAD)

    def send_coef(i, carry):
        g, h = slots_for(peer(gy, i, 1))
        first_half = jnp.where(g >= 0, coef_rows[jnp.maximum(g, 0)], 0.0)
        second_half = jnp.where(h >= 0, coef_rows[jnp.maximum(h, 0)], 0.0)
        c6s[i] = jnp.where(iota((8, 3 * PAD), 0) < GROUP, first_half, second_half)
        coef_copy(i).start()
        return carry
    lax.fori_loop(0, RAW, send_coef, 0)
    lax.fori_loop(WAVES[1], WAVES[2], send_raw, 0)
    x = iota((PAD, LANES), 1) % CRM_X

    def advance(read, speed, shift):
        s = padded(read(1))
        west = jnp.where(x == 0, pltpu.roll(s, LANES - 31, 1), pltpu.roll(s, 1, 1))
        east = jnp.where(x == CRM_X - 1, pltpu.roll(s, 31, 1), pltpu.roll(s, LANES - 1, 1))
        return (0.6 * s + 0.1 * ((east + west) + (padded(read(0)) + padded(read(2)))) - speed * (east - west)) + shift

    def physics(ref, i, lanes, speed, shift0, shift1):
        energy = advance(lambda k: ref[i, pl.ds(k, LEV), 0, lanes], speed, shift0)
        water = advance(lambda k: ref[i, pl.ds(k, LEV), 1, lanes], speed, shift1)
        base = 0.5 * energy + (1.25 * water - 0.625)
        half = base - 0.625 * jnp.tanh(0.5 * energy)
        half = base - 0.625 * jnp.tanh(half)
        half = base - 0.625 * jnp.tanh(half)
        return energy, 0.8 * water + (0.1 + 0.1 * jnp.tanh(half)), half

    def spread_out(i, slot):
        e = spread_of[:, pl.ds(pl.multiple_of(i * 256, 256), 256)]
        spread[slot] = dot(coef[0], e, NN) + dot(coef[1], e, NN)
    spread_out(0, 0)

    def two_groups(i, carry):
        slot = i % 2
        spread_out((i + 1) % (GROUPS // 2), (i + 1) % 2)
        for h in range(2):
            g = i * 2 + h
            c = slice(h * LANES, (h + 1) * LANES)
            energy, final, half = physics(
                crm, g, slice(None),
                spread[slot, 0:PAD, c], spread[slot, PAD:2 * PAD, c], spread[slot, 2 * PAD:3 * PAD, c])
            lanes = pl.ds(pl.multiple_of(g * LANES, LANES), LANES)
            warm[0, :, lanes] = half + half
            warm[1, :, lanes] = final
            fin[g, 0] = energy[0:LEV]
            fin[g, 1] = final[0:LEV]
        return carry
    lax.fori_loop(0, GROUPS // 2, two_groups, 0)

    def gather(i, d):
        for r, g in enumerate(slots_for(d)):
            block = fin[jnp.maximum(g, 0)]
            block = jnp.where(g >= 0, block, 0.0)
            for f in range(2):
                send[i, :, f, r * LANES:(r + 1) * LANES] = block[f]

    def send_final(i, carry):
        gather(i, peer(gy, i, 1))
        state_copy(i).start()
        return carry
    lax.fori_loop(WAVES[2], WAVES[3], send_final, 0)

    mean_sc[...] = jnp.zeros((2 * PAD, LANES), F32)

    def add_end(i, carry):
        lanes = pl.ds(pl.multiple_of(i * 512, 512), 512)
        hi, lo = split(jnp.concatenate([warm[0, :, lanes], warm[1, :, lanes]], axis=0), 2)
        e = spread_of[:, lanes]
        mean_sc[...] += dot(hi, e, NT) + dot(lo, e, NT)
        return carry
    lax.fori_loop(0, 8, add_end, 0)
    tendency = mean_sc[...] * (1.0 / CRM_X) - first
    back = hot((row // 8 == col % 32) & (row % 8 == col // 32))
    r1s[...] = pick_rows(back, tendency, NT).reshape(32, 8, LANES)[:, 0:NX]
    for i in range(NY - 1):
        tendency_copy(i).start()
    r1r[gy] = r1s[gy]

    lax.fori_loop(WAVES[3], NY - 1, send_final, 0)
    gather(31, gy)
    own = pltpu.make_async_copy(send.at[31], out_ref.at[:, :, own_lanes], own_sem)
    own.start()

    def take_coef(i, carry):
        coef_copy(i).wait()
        return carry
    lax.fori_loop(0, RAW, take_coef, 0)
    came = split(c6r[...].reshape(RAW * 8, 3 * PAD).T, 2)

    def finish(i, carry):
        raw_copy(i).wait()
        repeat_ends(raw, i)
        e = hot(iota((RAW * 8, 256), 0) == i * 8 + iota((RAW * 8, 256), 1) // CRM_X)
        both = dot(came[0], e, NN) + dot(came[1], e, NN)
        start = peer(gy, i, -1) * 256
        for r in range(2):
            c = both[:, r * LANES:(r + 1) * LANES]
            lanes = pl.ds(pl.multiple_of(start + r * LANES, LANES), LANES)
            energy, final, _ = physics(
                raw, i, slice(r * LANES, (r + 1) * LANES), c[0:PAD], c[PAD:2 * PAD], c[2 * PAD:3 * PAD])
            out_ref[:, 0, lanes] = energy[0:LEV]
            out_ref[:, 1, lanes] = (c[PAD - 1:PAD] * final)[0:LEV]
        return carry
    lax.fori_loop(0, RAW, finish, 0)

    for i in range(NY - 1):
        tendency_copy(i).wait()
    rows = iota((LANES, 256), 0)
    cols = iota((LANES, 256), 1)
    r2s[...] = pick_rows(
        hot((rows % 32 == cols // 8) & (rows // 32 == cols % 8)),
        jnp.concatenate([r1r[...], jnp.zeros((NY, 8 - NX, LANES), F32)], axis=1).reshape(256, LANES))
    stage4 = []
    for i, tx in enumerate(peers_x):
        copy = pltpu.make_async_remote_copy(
            src_ref=r2s.at[pl.ds(pl.multiple_of(tx * 32, 32), 32), :], dst_ref=r2r.at[own_rows, :],
            send_sem=s4.at[i], recv_sem=v4.at[i], device_id={"gx": tx}, device_id_type=MESH,
        )
        copy.start()
        stage4.append(copy)
    r2r[own_rows, :] = r2s[own_rows, :]

    for copy in stage4:
        copy.wait()
    placed = pick(r2r[...].T, chosen, NT)
    tend_ref[:, 0, :] = placed[0:LEV]
    tend_ref[:, 1, :] = placed[PAD:PAD + LEV]

    own.wait()

    def wait_final(i, carry):
        state_copy(i).wait()
        return carry
    lax.fori_loop(RAW, NY - 1, wait_final, 0)


PARTS = 8


def write_kernel(tend_ref, state_ref, tend_out, state_out, tend_sem, sems):
    tend = pltpu.make_async_copy(tend_ref, tend_out, tend_sem)
    copies = []
    for k in range(PARTS):
        lev = slice(k * 8, min(k * 8 + 8, LEV))
        copies.append(pltpu.make_async_copy(state_ref.at[lev], state_out.at[lev], sems.at[k]))
    for copy in copies + [tend]:
        copy.start()
    for copy in copies + [tend]:
        copy.wait()


def write_out(tendency, crm_next):
    vmem = pl.BlockSpec(memory_space=pltpu.VMEM)
    hbm = pl.BlockSpec(memory_space=pltpu.HBM)
    return pl.pallas_call(
        write_kernel,
        out_shape=(jax.ShapeDtypeStruct((LEV, 2, LANES), F32), jax.ShapeDtypeStruct((LEV, 2, 8192), F32)),
        in_specs=[vmem, vmem], out_specs=(hbm, hbm),
        scratch_shapes=[pltpu.SemaphoreType.DMA, pltpu.SemaphoreType.DMA((PARTS,))],
        compiler_params=pltpu.CompilerParams(vmem_limit_bytes=8 << 20),
    )(tendency, crm_next)


def on_device(gcm_state, crm_state, send_source, group_owner):
    vm = pltpu.VMEM
    dma = pltpu.SemaphoreType.DMA
    hbm = pl.BlockSpec(memory_space=pltpu.HBM)
    vmem = pl.BlockSpec(memory_space=pltpu.VMEM)
    crm_next, tendency = pl.pallas_call(
        step_kernel,
        out_shape=(jax.ShapeDtypeStruct((LEV, 2, 8192), F32), jax.ShapeDtypeStruct((LEV, 2, LANES), F32)),
        in_specs=[hbm] * 4,
        out_specs=(vmem, vmem),
        scratch_shapes=[
            vm((GROUPS, LEV + 2, 2, LANES), F32), vm((3, LEV, LANES), F32), vm((1, LANES), jnp.int32), vm((4, PAD, LANES), F32),
            vm((2, 128, LANES), F32), vm((2, 128, LANES), F32),
            vm((32, 8, LANES), F32), vm((32, 8, LANES), F32),
            vm((32, NX, LANES), F32), vm((32, NX, LANES), F32),
            vm((128, LANES), F32), vm((128, LANES), F32),
            vm((2, 3 * PAD, 256), F32), vm((LANES, 4096), BF16),
            vm((GROUPS, 2, LEV, LANES), F32), vm((2, PAD, 4096), F32),
            vm((32, LEV, 2, 256), F32), vm((2 * PAD, LANES), F32), vm((2, 3 * PAD, LANES), BF16),
            vm((RAW, 8, 3 * PAD), F32), vm((RAW, 8, 3 * PAD), F32), vm((GROUPS, 8, 3 * PAD), F32), vm((RAW, LEV + 2, 2, 256), F32),
            pltpu.SMEM((GROUPS,), jnp.int32), dma((GROUPS,)), dma, dma, dma, dma, dma((3,)), dma((3,)), dma((31,)), dma((31,)), dma((31,)), dma((31,)),
            dma((3,)), dma((3,)), dma((31,)), dma((31,)), dma((RAW,)), dma((RAW,)),
        ],
        compiler_params=pltpu.CompilerParams(collective_id=0, has_side_effects=True, vmem_limit_bytes=48 << 20),
    )(*[pltpu.with_memory_space_constraint(a, pltpu.HBM) for a in (
        group_owner, send_source.reshape(1, LANES), gcm_state, crm_state.transpose(1, 0, 2))])
    tendency, crm_next = write_out(tendency, crm_next)
    return tendency.transpose(1, 0, 2), crm_next.transpose(1, 0, 2)


def solution(mesh):
    spec = P(None, None, ("gx", "gy"))
    flat = P(("gx", "gy"))
    return jax.shard_map(
        on_device, mesh=mesh, in_specs=(spec, spec, flat, flat), out_specs=(spec, spec), check_vma=False)
```
